512 devices in a mesh: sx: 8 (over x, core), sy: 8 (over z), dir: 8 (over y).
Axes of the slice: x: 4, y: 8, z: 8, core: 2. Of those that a mesh axis runs over, the one named last changes fastest.
Arguments:
- directions: float32 [7, 64, 16, 64, 128], P(None, 'dir', 'sx', 'sy'), may hold values from -6 to 6
- conductance: float32 [7, 16, 64, 128], P(None, 'sx', 'sy'), may hold values from 0.2 to 0.4
- diag_inverse: float32 [7, 16, 64, 128], P(None, 'sx', 'sy'), may hold values from 0.3 to 0.9
- cross_inverse: float32 [7, 7, 16, 64, 128], P(None, None, 'sx', 'sy'), may hold values from -0.5 to 0.5
- coupling: int32 [7, 7], replicated, may hold values 0 or 1
- sensitivity: float32 [7, 16, 64, 128], P(None, 'sx', 'sy'), may hold values from -6 to 6
- obs_weight: float32 [7, 16, 64, 128], P(None, 'sx', 'sy'), may hold values from 0.3 to 3
- prior_weight: float32 [7, 16, 64, 128], P(None, 'sx', 'sy'), may hold values from 0.1 to 0.5
Outputs:
- hess_action: float32 [7, 64, 16, 64, 128], P(None, 'dir', 'sx', 'sy')
- r_factor: float32 [64, 64], replicated
The draws below stay inside these ranges and needn't reach their ends.
All inputs are finite; a program needn't handle non-finite values.
Results may differ from the reference program's by a relative error of at most 0.0002.
Values sent between devices are 32-bit elements; how exact they have to be, the bound alone decides.
No kernel may reach another device: no remote copies, remote signals or barrier semaphores. Data moves between devices by JAX's collectives and lax.ppermute only.
A program may use at most 64 MiB of HBM per device.

```python
import math
import jax
import jax.numpy as jnp
from jax import lax

SPEC = 7
KDEV = 8
SWEEPS = 4
NZ = 128
KDIR = 64
NX = 16
NY = 64
ROWS = 917504
N_DIR = 8


def place_ends(values, own_key, least, top_value):
    longest = values.shape.index(max(values.shape))
    spots = []
    for shift in (0, 1):
        where = [jax.random.randint(jax.random.fold_in(own_key, axis), (), 0, length) for axis, length in enumerate(values.shape)]
        where[longest] = (where[longest] + shift) % values.shape[longest]
        spots.append(tuple(where))
    return values.at[spots[0]].set(least).at[spots[1]].set(top_value)


def block_scale(own_key, extent, shards, low, high):
    gain = 1.0
    for dim, parts in shards:
        draws = jax.random.uniform(jax.random.fold_in(jax.random.fold_in(own_key, 6), dim), (parts,), jnp.float32, low / len(shards), high / len(shards))
        gain = gain * jnp.repeat(jnp.exp(draws), extent[dim] // parts).reshape((-1,) + (1,) * (len(extent) - 1 - dim))
    return gain


def noise(rng, extent, scale, bound, pieces=(), kind=jnp.bfloat16):
    values = scale * jax.random.normal(rng, extent, jnp.float32)
    if pieces:
        values = values * block_scale(rng, extent, pieces, -0.22, 0.18)
    return jnp.clip(values, -bound, bound).astype(kind)


def setup_inputs(seed: int = 0) -> dict:
    key_of = jax.random.split(jax.random.key(seed), 9)
    return {
        "directions": noise(key_of[0], (SPEC, KDIR, NX, NY, NZ), 1.0, 6.0, ((1, 8), (2, 8), (3, 8)), jnp.float32),
        "conductance": jnp.clip(jnp.exp(math.log(0.4) - 0.6931472 * jax.random.uniform(key_of[1], (SPEC, NX, NY, NZ), jnp.float32) ** block_scale(key_of[1], (SPEC, NX, NY, NZ), ((1, 8), (2, 8)), -0.2, 0.2)), 0.2, 0.4),
        "diag_inverse": jnp.clip(jnp.exp(math.log(0.9) - 1.0986122 * jax.random.uniform(key_of[2], (SPEC, NX, NY, NZ), jnp.float32) ** block_scale(key_of[2], (SPEC, NX, NY, NZ), ((1, 8), (2, 8)), -0.2, 0.2)), 0.3, 0.9),
        "cross_inverse": noise(key_of[3], (SPEC, SPEC, NX, NY, NZ), 0.12, 0.5, ((2, 8), (3, 8)), jnp.float32),
        "coupling": place_ends((jax.random.randint(key_of[4], (SPEC, SPEC), 0, 2) < 1).astype(jnp.int32), jax.random.fold_in(key_of[4], 1), 0, 1),
        "sensitivity": noise(key_of[5], (SPEC, NX, NY, NZ), 1.0, 6.0, ((1, 8), (2, 8)), jnp.float32),
        "obs_weight": jnp.clip(jnp.exp(math.log(3.0) - 2.3025851 * jax.random.uniform(key_of[6], (SPEC, NX, NY, NZ), jnp.float32) ** block_scale(key_of[6], (SPEC, NX, NY, NZ), ((1, 8), (2, 8)), -0.2, 0.2)), 0.3, 3.0),
        "prior_weight": jnp.clip(jnp.exp(math.log(0.5) - 1.609438 * jax.random.uniform(key_of[7], (SPEC, NX, NY, NZ), jnp.float32) ** block_scale(key_of[7], (SPEC, NX, NY, NZ), ((1, 8), (2, 8)), -0.2, 0.2)), 0.1, 0.5),
    }


def apply_block(diag_inverse, cross_eff, source, transpose):
    result = diag_inverse[:, None] * source
    for species in range(source.shape[0]):
        column = cross_eff[species] if transpose else cross_eff[:, species]
        result = result + column[:, None] * source[species][None]
    return result

def neighbour_sum(fluxes):
    zeros_x = jnp.zeros_like(fluxes[..., :1, :, :])
    forward_x = jnp.concatenate([fluxes[..., 1:, :, :], zeros_x], axis=-3)
    backward_x = jnp.concatenate([zeros_x, fluxes[..., :-1, :, :]], axis=-3)
    forward_y = jnp.roll(fluxes, -1, axis=-2)
    backward_y = jnp.roll(fluxes, 1, axis=-2)
    zeros_z = jnp.zeros_like(fluxes[..., :1])
    forward_z = jnp.concatenate([fluxes[..., 1:], zeros_z], axis=-1)
    backward_z = jnp.concatenate([zeros_z, fluxes[..., :-1]], axis=-1)
    return forward_x + backward_x + forward_y + backward_y + forward_z + backward_z

def jacobi(rhs, conductance, diag_inverse, cross_eff, transpose):
    current = apply_block(diag_inverse, cross_eff, rhs, transpose)
    for sweep_index in range(SWEEPS - 1):
        fluxes = conductance[:, None] * current
        source = rhs + conductance[:, None] * neighbour_sum(fluxes)
        current = apply_block(diag_inverse, cross_eff, source, transpose)
    return current

def reference(directions, conductance, diag_inverse, cross_inverse, coupling, sensitivity, obs_weight, prior_weight):
    offdiag = coupling.astype(jnp.float32) * (1.0 - jnp.eye(SPEC, dtype=jnp.float32))
    cross_eff = cross_inverse * offdiag[:, :, None, None, None]

    def one_group(group):
        dir_block = lax.dynamic_slice_in_dim(directions, group * KDEV, KDEV, 1)
        forward = jacobi(sensitivity[:, None] * dir_block, conductance, diag_inverse, cross_eff, False)
        adjoint = jacobi(obs_weight[:, None] * forward, conductance, diag_inverse, cross_eff, True)
        return sensitivity[:, None] * adjoint + prior_weight[:, None] * dir_block
    groups = lax.map(one_group, jnp.arange(N_DIR, dtype=jnp.int32))
    hess_action = jnp.moveaxis(groups, 0, 1).reshape(SPEC, KDIR, NX, NY, NZ)
    gram = jnp.einsum('sdxyz,sexyz->de', hess_action, hess_action, precision=lax.Precision.HIGHEST) / ROWS
    r_factor = jnp.linalg.cholesky(gram).T
    return (hess_action, r_factor)
```

```python
import functools

import jax
import jax.numpy as jnp
from jax import lax
from jax.experimental import pallas as pl
from jax.experimental.pallas import tpu as pltpu
from jax.sharding import PartitionSpec as P

SPEC = 7
KDEV = 8
LX = 2
LY = 8
NZ = 128
PAIRS = SPEC * LX
F32 = jnp.float32


def row(ref, index):
    return jnp.broadcast_to(ref[pl.ds(index, 1), :], (KDEV, NZ))


def block_terms(beff, source, cell, transpose):
    out = []
    for s in range(SPEC):
        total = row(beff, (s * SPEC + s) * LX * LY + cell) * source[s]
        for t in range(SPEC):
            if t != s:
                entry = t * SPEC + s if transpose else s * SPEC + t
                total = total + row(beff, entry * LX * LY + cell) * source[t]
        out.append(total)
    return out


def parities():
    return lax.rem(lax.axis_index("sx"), 2), lax.rem(lax.axis_index("sy"), 2)


def store_sends(flux, cross, inside, ya, yb):
    px, py = parities()
    cross[...] = flux[:, px]
    inside[...] = flux[:, 1 - px]
    ya[...] = flux[:, :, 7 * (1 - py)]
    yb[...] = flux[:, :, 7 * py]


def first_kernel(dirs, cond, diag, crossinv, coup, sens, beff, rhs, flux, cross, inside, ya, yb):
    for s in range(SPEC):
        for t in range(SPEC):
            here = pl.ds((s * SPEC + t) * LX * LY, LX * LY)
            if s == t:
                beff[here, :] = diag[pl.ds(s * LX * LY, LX * LY), :]
            else:
                beff[here, :] = crossinv[here, :] * coup[s, t].astype(F32)

    def body(y, carry):
        for x in range(LX):
            cell = x * LY + y
            source = []
            for s in range(SPEC):
                d = dirs[pl.ds(s * KDEV * LX * LY + cell, KDEV, stride=LX * LY), :]
                r = row(sens, s * LX * LY + cell) * d
                rhs[s, x, y] = r
                source.append(r)
            values = block_terms(beff, source, cell, False)
            for s in range(SPEC):
                flux[s, x, y] = row(cond, s * LX * LY + cell) * values[s]
        return carry

    lax.fori_loop(0, LY, body, 0)
    store_sends(flux, cross, inside, ya, yb)


def fill_wide(wide, flux, rcross, rinside, rya, ryb):
    px, py = parities()
    wide[:, 1:3, 1:9] = flux[...]
    wide[:, 3 * px, 1:9] = rcross[...]
    wide[:, 3 * (1 - px), 1:9] = rinside[...]
    wide[:, 1:3, 9 * (1 - py)] = rya[...]
    wide[:, 1:3, 9 * py] = ryb[...]


def source_terms(wide, rhs, cond, x, y, cell, lane):
    source = []
    for s in range(SPEC):
        centre = wide[s, x + 1, y + 1]
        total = wide[s, x + 2, y + 1] + wide[s, x, y + 1]
        total = total + wide[s, x + 1, y + 2]
        total = total + wide[s, x + 1, y]
        total = total + jnp.where(lane == NZ - 1, 0.0, pltpu.roll(centre, NZ - 1, 1))
        total = total + jnp.where(lane == 0, 0.0, pltpu.roll(centre, 1, 1))
        source.append(rhs[s, x, y] + row(cond, s * LX * LY + cell) * total)
    return source


def sweep_kernel(transpose, fluxin, rcross, rinside, rya, ryb, rhs, beff, cond,
                 flux, cross, inside, ya, yb, wide):
    fill_wide(wide, fluxin, rcross, rinside, rya, ryb)
    lane = lax.broadcasted_iota(jnp.int32, (KDEV, NZ), 1)

    def body(y, carry):
        for x in range(LX):
            cell = x * LY + y
            source = source_terms(wide, rhs, cond, x, y, cell, lane)
            values = block_terms(beff, source, cell, transpose)
            for s in range(SPEC):
                flux[s, x, y] = row(cond, s * LX * LY + cell) * values[s]
        return carry

    lax.fori_loop(0, LY, body, 0)
    store_sends(flux, cross, inside, ya, yb)


def turn_kernel(fluxin, rcross, rinside, rya, ryb, rhs, beff, cond, obs,
                rhs2, flux, cross, inside, ya, yb, wide):
    fill_wide(wide, fluxin, rcross, rinside, rya, ryb)
    lane = lax.broadcasted_iota(jnp.int32, (KDEV, NZ), 1)

    def body(y, carry):
        for x in range(LX):
            cell = x * LY + y
            source = source_terms(wide, rhs, cond, x, y, cell, lane)
            forward = block_terms(beff, source, cell, False)
            second = []
            for s in range(SPEC):
                r = row(obs, s * LX * LY + cell) * forward[s]
                rhs2[s, x, y] = r
                second.append(r)
            values = block_terms(beff, second, cell, True)
            for s in range(SPEC):
                flux[s, x, y] = row(cond, s * LX * LY + cell) * values[s]
        return carry

    lax.fori_loop(0, LY, body, 0)
    store_sends(flux, cross, inside, ya, yb)


def last_kernel(fluxin, rcross, rinside, rya, ryb, rhs, beff, cond, sens, prior, dirs,
                hess, spread, wide):
    fill_wide(wide, fluxin, rcross, rinside, rya, ryb)
    lane = lax.broadcasted_iota(jnp.int32, (KDEV, NZ), 1)

    def body(y, carry):
        for x in range(LX):
            cell = x * LY + y
            source = source_terms(wide, rhs, cond, x, y, cell, lane)
            values = block_terms(beff, source, cell, True)
            for s in range(SPEC):
                rows = pl.ds(s * KDEV * LX * LY + cell, KDEV, stride=LX * LY)
                h = row(sens, s * LX * LY + cell) * values[s]
                h = h + row(prior, s * LX * LY + cell) * dirs[rows, :]
                hess[rows, :] = h
                spread[y, :, pl.ds((s * LX + x) * NZ, NZ)] = h
        return carry

    lax.fori_loop(0, LY, body, 0)


def gram_kernel(scale, actions, out):
    a = actions[...]
    gram = lax.dot_general(
        a, a, (((1,), (1,)), ((), ())),
        precision=lax.Precision.HIGHEST, preferred_element_type=F32,
    ) * scale
    packed = jnp.concatenate([gram[:32], gram[32:]], axis=1)
    for k in range(8):
        out[k] = packed


def reduce_kernel(parts, out):
    total = parts[0]
    for k in range(1, 8):
        total = total + parts[k]
    for k in range(8):
        out[k] = total


def unpack_kernel(parts, out):
    total = parts[0]
    for k in range(1, 8):
        total = total + parts[k]
    out[...] = jnp.concatenate([total[:, :64], total[:, 64:]], axis=0)


def call(body, out_shapes, smem=(), scratch=(), flops=1000, name=None):
    def run(*args):
        vmem = pl.BlockSpec(memory_space=pltpu.VMEM)
        specs = [
            pl.BlockSpec(memory_space=pltpu.SMEM) if i in smem else vmem
            for i in range(len(args))
        ]
        return pl.pallas_call(
            body,
            out_shape=[jax.ShapeDtypeStruct(s, F32) for s in out_shapes],
            in_specs=specs,
            out_specs=[vmem] * len(out_shapes),
            scratch_shapes=list(scratch),
            compiler_params=pltpu.CompilerParams(vmem_limit_bytes=12 << 20),
            name=name,
        )(*args)

    return run


STATE = (SPEC, LX, LY, KDEV, NZ)
SENDS = [(SPEC, LY, KDEV, NZ)] * 2 + [(SPEC, LX, KDEV, NZ)] * 2
WIDE = pltpu.VMEM((SPEC, LX + 2, LY + 2, KDEV, NZ), F32)


def exchange(cross, inside, ya, yb):
    nx, ny = lax.axis_size("sx"), lax.axis_size("sy")
    inner = [(i, i ^ 1) for i in range(nx)]
    outer = [(i, i + 1 if i % 2 else i - 1) for i in range(1, nx - 1)]
    even = [(i, i ^ 1) for i in range(ny)]
    odd = [(i, (i + 1) % ny if i % 2 else (i - 1) % ny) for i in range(ny)]
    return (
        lax.ppermute(cross, "sx", outer),
        lax.ppermute(inside, "sx", inner),
        lax.ppermute(ya, "sy", even),
        lax.ppermute(yb, "sy", odd),
    )


def local(dirs, cond, diag, crossinv, coup, sens, obs, prior):
    flat = lambda a: a.reshape(-1, NZ)
    hess_shape = dirs.shape
    dirs, cond, diag, crossinv, sens, obs, prior = map(
        flat, (dirs, cond, diag, crossinv, sens, obs, prior)
    )
    beff, rhs, flux, *sends = call(
        first_kernel, [(SPEC * SPEC * LX * LY, NZ), STATE, STATE] + SENDS, smem=(4,), name="first"
    )(dirs, cond, diag, crossinv, coup, sens)
    sweep = lambda transpose: call(
        functools.partial(sweep_kernel, transpose), [STATE] + SENDS, scratch=[WIDE], name="sweep"
    )
    for _ in range(2):
        flux, *sends = sweep(False)(flux, *exchange(*sends), rhs, beff, cond)
    rhs, flux, *sends = call(turn_kernel, [STATE, STATE] + SENDS, scratch=[WIDE], name="turn")(
        flux, *exchange(*sends), rhs, beff, cond, obs
    )
    for _ in range(2):
        flux, *sends = sweep(True)(flux, *exchange(*sends), rhs, beff, cond)
    hess, spread = call(
        last_kernel, [dirs.shape, (LY, KDEV, PAIRS * NZ)], scratch=[WIDE], name="last"
    )(flux, *exchange(*sends), rhs, beff, cond, sens, prior, dirs)

    gathered = lax.all_to_all(spread, "dir", split_axis=0, concat_axis=0, tiled=True)
    gathered = gathered.reshape(8 * KDEV, PAIRS * NZ)
    rows = SPEC * LX * LY * NZ * lax.axis_size("sx") * lax.axis_size("sy")
    (parts,) = call(functools.partial(gram_kernel, 1.0 / rows), [(8, 32, 128)], name="gram")(gathered)
    parts = lax.all_to_all(parts, "sx", split_axis=0, concat_axis=0, tiled=True)
    (parts,) = call(reduce_kernel, [(8, 32, 128)], name="reduce_sx")(parts)
    parts = lax.all_to_all(parts, "sy", split_axis=0, concat_axis=0, tiled=True)
    (parts,) = call(reduce_kernel, [(8, 32, 128)], name="reduce_sy")(parts)
    parts = lax.all_to_all(parts, "dir", split_axis=0, concat_axis=0, tiled=True)
    (gram,) = call(unpack_kernel, [(64, 64)], name="unpack")(parts)
    r_factor = jnp.linalg.cholesky(gram).T
    return hess.reshape(hess_shape), r_factor


def solution(mesh):
    cells = P(None, "sx", "sy", None)
    return jax.shard_map(
        local,
        mesh=mesh,
        in_specs=(
            P(None, "dir", "sx", "sy", None), cells, cells,
            P(None, None, "sx", "sy", None), P(), cells, cells, cells,
        ),
        out_specs=(P(None, "dir", "sx", "sy", None), P()),
        check_vma=False,
    )
```

```python
import functools

import jax
import jax.numpy as jnp
from jax import lax
from jax.experimental import pallas as pl
from jax.experimental.pallas import tpu as pltpu
from jax.sharding import PartitionSpec as P


SPEC = 7
KDEV = 8
LX = 2
LY = 8
NZ = 128
PAIRS = SPEC * LX
F32 = jnp.float32


def row(ref, index):
    return jnp.broadcast_to(ref[pl.ds(index, 1), :], (KDEV, NZ))


def block_terms(beff, source, cell, transpose):
    out = []
    for s in range(SPEC):
        total = row(beff, (s * SPEC + s) * LX * LY + cell) * source[s]
        for t in range(SPEC):
            if t != s:
                entry = t * SPEC + s if transpose else s * SPEC + t
                total = total + row(beff, entry * LX * LY + cell) * source[t]
        out.append(total)
    return out


def parities():
    return lax.rem(lax.axis_index("sx"), 2), lax.rem(lax.axis_index("sy"), 2)


def pick(first, a, b):
    return jnp.where(first, a, b), jnp.where(first, b, a)


def store_x(cross, inside, y, pairs):
    even = parities()[0] == 0
    for s in range(SPEC):
        cross[s, y], inside[s, y] = pick(even, *pairs[s])


def store_y(flux, ya, yb):
    py = parities()[1]
    ya[...] = flux[:, :, 7 * (1 - py)]
    yb[...] = flux[:, :, 7 * py]


def first_kernel(dirs_hbm, cond_hbm, diag_hbm, crossinv_hbm, coup_hbm, sens_hbm,
                 beff, rhs, flux, cross, inside, ya, yb,
                 dirs, cond, diag, crossinv, coup, sens, sems):
    sources = (coup_hbm, diag_hbm, crossinv_hbm, dirs_hbm, cond_hbm, sens_hbm)
    targets = (coup, diag, crossinv, dirs, cond, sens)
    copies = [
        pltpu.make_async_copy(source, target, sems.at[k])
        for k, (source, target) in enumerate(zip(sources, targets))
    ]
    for copy in copies:
        copy.start()
    for copy in copies[:3]:
        copy.wait()
    links = coup[...].astype(F32)
    for s in range(SPEC):
        for t in range(SPEC):
            here = pl.ds((s * SPEC + t) * LX * LY, LX * LY)
            if s == t:
                beff[here, :] = diag[pl.ds(s * LX * LY, LX * LY), :]
            else:
                link = jnp.broadcast_to(links[s : s + 1, t : t + 1], (LX * LY, NZ))
                beff[here, :] = crossinv[here, :] * link
    for copy in copies[3:]:
        copy.wait()

    def body(y, carry):
        pairs = [[] for _ in range(SPEC)]
        for x in range(LX):
            cell = x * LY + y
            source = []
            for s in range(SPEC):
                d = dirs[pl.ds(s * KDEV * LX * LY + cell, KDEV, stride=LX * LY), :]
                r = row(sens, s * LX * LY + cell) * d
                rhs[s, x, y] = r
                source.append(r)
            values = block_terms(beff, source, cell, False)
            for s in range(SPEC):
                f = row(cond, s * LX * LY + cell) * values[s]
                flux[s, x, y] = f
                pairs[s].append(f)
        store_x(cross, inside, y, pairs)
        return carry

    lax.fori_loop(0, LY, body, 0, unroll=4)
    store_y(flux, ya, yb)


def inner_kernel(flux, rhs, cond, part):
    lane = lax.broadcasted_iota(jnp.int32, (KDEV, NZ), 1)

    def cells(y):
        for x in range(LX):
            cell = x * LY + y
            for s in range(SPEC):
                centre = flux[s, x, y]
                total = flux[s, 1 - x, y]
                if not isinstance(y, int) or y < LY - 1:
                    total = total + flux[s, x, y + 1]
                if not isinstance(y, int) or y > 0:
                    total = total + flux[s, x, y - 1]
                total = total + jnp.where(lane == NZ - 1, 0.0, pltpu.roll(centre, NZ - 1, 1))
                total = total + jnp.where(lane == 0, 0.0, pltpu.roll(centre, 1, 1))
                part[s, x, y] = rhs[s, x, y] + row(cond, s * LX * LY + cell) * total

    def body(y, carry):
        cells(y)
        return carry

    cells(0)
    lax.fori_loop(1, LY - 1, body, 0, unroll=3)
    cells(LY - 1)


def with_halos(part, rcross, rinside, rya, ryb, cond, finish):
    px, py = parities()
    even_x, even_y = px == 0, py == 0

    def cells(y):
        sides = [pick(even_x, rcross[s, y], rinside[s, y]) for s in range(SPEC)]
        done = []
        for x in range(LX):
            cell = x * LY + y
            source = []
            for s in range(SPEC):
                halo = sides[s][x]
                if isinstance(y, int):
                    upper, lower = pick(even_y, rya[s, x], ryb[s, x])
                    halo = halo + (lower if y == 0 else upper)
                source.append(part[s, x, y] + row(cond, s * LX * LY + cell) * halo)
            done.append(finish(x, y, cell, source))
        return done

    return cells


def run_cells(cells, after):
    def body(y, carry):
        after(y, cells(y))
        return carry

    after(0, cells(0))
    lax.fori_loop(1, LY - 1, body, 0, unroll=3)
    after(LY - 1, cells(LY - 1))


def sweep_kernel(transpose, part, rcross, rinside, rya, ryb, beff, cond,
                 flux, cross, inside, ya, yb):
    def finish(x, y, cell, source):
        values = block_terms(beff, source, cell, transpose)
        out = []
        for s in range(SPEC):
            f = row(cond, s * LX * LY + cell) * values[s]
            flux[s, x, y] = f
            out.append(f)
        return out

    run_cells(
        with_halos(part, rcross, rinside, rya, ryb, cond, finish),
        lambda y, done: store_x(cross, inside, y, list(zip(*done))),
    )
    store_y(flux, ya, yb)


def turn_kernel(part, rcross, rinside, rya, ryb, beff, cond, obs,
                rhs2, flux, cross, inside, ya, yb):
    def finish(x, y, cell, source):
        forward = block_terms(beff, source, cell, False)
        second = []
        for s in range(SPEC):
            r = row(obs, s * LX * LY + cell) * forward[s]
            rhs2[s, x, y] = r
            second.append(r)
        values = block_terms(beff, second, cell, True)
        out = []
        for s in range(SPEC):
            f = row(cond, s * LX * LY + cell) * values[s]
            flux[s, x, y] = f
            out.append(f)
        return out

    run_cells(
        with_halos(part, rcross, rinside, rya, ryb, cond, finish),
        lambda y, done: store_x(cross, inside, y, list(zip(*done))),
    )
    store_y(flux, ya, yb)


def last_kernel(part, rcross, rinside, rya, ryb, beff, cond, sens, prior, dirs,
                hess, spread):
    def finish(x, y, cell, source):
        values = block_terms(beff, source, cell, True)
        for s in range(SPEC):
            rows = pl.ds(s * KDEV * LX * LY + cell, KDEV, stride=LX * LY)
            h = row(sens, s * LX * LY + cell) * values[s]
            h = h + row(prior, s * LX * LY + cell) * dirs[rows, :]
            hess[rows, :] = h
            spread[y, :, pl.ds((s * LX + x) * NZ, NZ)] = h

    run_cells(with_halos(part, rcross, rinside, rya, ryb, cond, finish), lambda y, done: None)


def gram_kernel(scale, actions, out):
    a = actions[...]
    gram = lax.dot_general(
        a, a, (((1,), (1,)), ((), ())),
        precision=lax.Precision.HIGHEST, preferred_element_type=F32,
    ) * scale
    top = jnp.concatenate([gram[:16], gram[16:32]], axis=1)
    corner = jnp.concatenate([gram[32 + 8 * k : 40 + 8 * k, 32:] for k in range(4)], axis=1)
    for k in range(8):
        out[k, :16] = top
        out[k, 16:] = corner


def reduce_kernel(parts, out):
    total = parts[0]
    for k in range(1, 8):
        total = total + parts[k]
    for k in range(8):
        out[k] = total


def finish_kernel(parts, hess, hess_hbm, out, rows, cols, sem):
    write = pltpu.make_async_copy(hess, hess_hbm, sem.at[0])
    write.start()
    cholesky_steps(parts, out, rows, cols)
    write.wait()


def cholesky_steps(parts, out, rows, cols):
    total = parts[0]
    for k in range(1, 8):
        total = total + parts[k]
    blocks = [total[:8, :64], total[8:16, :64], total[:8, 64:], total[8:16, 64:]]
    right = jnp.concatenate([block[:, 32:] for block in blocks], axis=0)
    eye = (
        lax.broadcasted_iota(jnp.int32, (32, 32), 0) == lax.broadcasted_iota(jnp.int32, (32, 32), 1)
    ).astype(F32)
    left = lax.dot_general(
        right, eye, (((0,), (0,)), ((), ())),
        precision=lax.Precision.HIGHEST, preferred_element_type=F32,
    )
    for k in range(4):
        corner = total[16:24, 32 * k : 32 * k + 32]
        blocks.append(jnp.concatenate([left[8 * k : 8 * k + 8], corner], axis=1))
    lane = lax.broadcasted_iota(jnp.int32, (8, 64), 1)
    for b in range(8):
        rows[...] = blocks[b]
        wide = {}
        for c in range(b, 8):
            for i in range(8):
                pivot = 8 * b + i
                wide[c, i] = jnp.broadcast_to(blocks[c][:, pivot : pivot + 1], (8, 64))
        for i in range(8):
            cols[i] = wide[b, i]
        entry = {
            (i, j): jnp.broadcast_to(cols[i, pl.ds(j, 1), :], (8, 64))
            for i in range(8) for j in range(i, 8)
        }
        full = [jnp.broadcast_to(rows[pl.ds(i, 1), :], (8, 64)) for i in range(8)]
        for i in range(8):
            inverse = lax.rsqrt(entry[i, i])
            for j in range(i + 1, 8):
                entry[i, j] = entry[i, j] * inverse
            full[i] = full[i] * inverse
            for c in range(b + 1, 8):
                wide[c, i] = wide[c, i] * inverse
            for j in range(i + 1, 8):
                for l in range(j, 8):
                    entry[j, l] = entry[j, l] - entry[i, j] * entry[i, l]
                full[j] = full[j] - entry[i, j] * full[i]
                for c in range(b + 1, 8):
                    wide[c, j] = wide[c, j] - entry[i, j] * wide[c, i]
            pivot = 8 * b + i
            out[pl.ds(pivot, 1), :] = jnp.where(lane >= pivot, full[i], 0.0)[:1]
            for c in range(b + 1, 8):
                blocks[c] = blocks[c] - wide[c, i] * full[i]


def call(body, out_shapes, hbm_in=(), hbm_out=(), scratch=()):
    def run(*args):
        vmem = pl.BlockSpec(memory_space=pltpu.VMEM)
        hbm = pl.BlockSpec(memory_space=pltpu.MemorySpace.HBM)
        return pl.pallas_call(
            body,
            out_shape=[jax.ShapeDtypeStruct(s, F32) for s in out_shapes],
            in_specs=[hbm if i in hbm_in else vmem for i in range(len(args))],
            out_specs=[hbm if i in hbm_out else vmem for i in range(len(out_shapes))],
            scratch_shapes=list(scratch),
            compiler_params=pltpu.CompilerParams(vmem_limit_bytes=12 << 20),
        )(*args)

    return run


STATE = (SPEC, LX, LY, KDEV, NZ)
SENDS = [(SPEC, LY, KDEV, NZ)] * 2 + [(SPEC, LX, KDEV, NZ)] * 2


ORDER = ("yodd", "cross", "yeven", "inside")


def exchange(cross, inside, ya, yb):
    nx, ny = lax.axis_size("sx"), lax.axis_size("sy")
    inner = [(i, i ^ 1) for i in range(nx)]
    outer = [(i, i + 1 if i % 2 else i - 1) for i in range(1, nx - 1)]
    even = [(i, i ^ 1) for i in range(ny)]
    odd = [(i, (i + 1) % ny if i % 2 else (i - 1) % ny) for i in range(ny)]
    moves = {
        "cross": (cross, "sx", outer), "inside": (inside, "sx", inner),
        "yeven": (ya, "sy", even), "yodd": (yb, "sy", odd),
    }
    got = {}
    for key in ORDER:
        got[key] = lax.ppermute(*moves[key])
    return got["cross"], got["inside"], got["yeven"], got["yodd"]


def local(dirs, cond, diag, crossinv, coup, sens, obs, prior):
    flat = lambda a: a.reshape(-1, NZ)
    hess_shape = dirs.shape
    dirs, cond, diag, crossinv, sens, obs, prior = map(
        flat, (dirs, cond, diag, crossinv, sens, obs, prior)
    )
    beff, rhs, flux, *sends = call(
        first_kernel, [(SPEC * SPEC * LX * LY, NZ), STATE, STATE] + SENDS, hbm_in=range(6),
        scratch=[
            pltpu.VMEM(dirs.shape, F32), pltpu.VMEM(cond.shape, F32), pltpu.VMEM(diag.shape, F32),
            pltpu.VMEM(crossinv.shape, F32), pltpu.VMEM(coup.shape, jnp.int32),
            pltpu.VMEM(sens.shape, F32), pltpu.SemaphoreType.DMA((6,)),
        ],
    )(*(pltpu.with_memory_space_constraint(a, pltpu.MemorySpace.HBM)
        for a in (dirs, cond, diag, crossinv, coup, sens)))

    def inner(flux, rhs):
        (part,) = call(inner_kernel, [STATE])(flux, rhs, cond)
        return part

    sweep = lambda transpose: call(
        functools.partial(sweep_kernel, transpose), [STATE] + SENDS
    )
    for _ in range(2):
        part, halos = inner(flux, rhs), exchange(*sends)
        flux, *sends = sweep(False)(part, *halos, beff, cond)
    part, halos = inner(flux, rhs), exchange(*sends)
    rhs, flux, *sends = call(turn_kernel, [STATE, STATE] + SENDS)(
        part, *halos, beff, cond, obs
    )
    for _ in range(3, 5):
        part, halos = inner(flux, rhs), exchange(*sends)
        flux, *sends = sweep(True)(part, *halos, beff, cond)
    part, halos = inner(flux, rhs), exchange(*sends)
    hess, spread = call(last_kernel, [dirs.shape, (LY, KDEV, PAIRS * NZ)])(
        part, *halos, beff, cond, sens, prior, dirs
    )

    gathered = lax.all_to_all(spread, "dir", split_axis=0, concat_axis=0, tiled=True)
    gathered = gathered.reshape(8 * KDEV, PAIRS * NZ)
    rows = SPEC * LX * LY * NZ * lax.axis_size("sx") * lax.axis_size("sy")
    (parts,) = call(functools.partial(gram_kernel, 1.0 / rows), [(8, 24, 128)])(gathered)
    parts = lax.all_to_all(parts, "sx", split_axis=0, concat_axis=0, tiled=True)
    (parts,) = call(reduce_kernel, [(8, 24, 128)])(parts)
    parts = lax.all_to_all(parts, "sy", split_axis=0, concat_axis=0, tiled=True)
    (parts,) = call(reduce_kernel, [(8, 24, 128)])(parts)
    parts = lax.all_to_all(parts, "dir", split_axis=0, concat_axis=0, tiled=True)
    hess, r_factor = call(
        finish_kernel, [dirs.shape, (64, 64)], hbm_out=(0,),
        scratch=[
            pltpu.VMEM((8, 64), F32), pltpu.VMEM((8, 8, 64), F32),
            pltpu.SemaphoreType.DMA((1,)),
        ],
    )(parts, hess)
    return hess.reshape(hess_shape), r_factor


def solution(mesh):
    cells = P(None, "sx", "sy", None)

    return jax.shard_map(
        local,
        mesh=mesh,
        in_specs=(
            P(None, "dir", "sx", "sy", None), cells, cells,
            P(None, None, "sx", "sy", None), P(), cells, cells, cells,
        ),
        out_specs=(P(None, "dir", "sx", "sy", None), P()),
        check_vma=False,
    )
```
